512 devices in a mesh: expert: 128 (over x, z_lo, y), dp: 4 (over z_hi, core).
Axes of the slice: x: 4, y: 4, z: 16 (z_hi: 2, z_lo: 8; z = z_hi * 8 + z_lo), core: 2. Of those that a mesh axis runs over, the one named last changes fastest.
Arguments:
- tokens: bfloat16 [8192, 2048], P(('expert', 'dp')), may hold values from -6 to 6
- cotangent: bfloat16 [8192, 2048], P(('expert', 'dp')), may hold values from -6 to 6
- route_ids: int32 [8192, 8], P(('expert', 'dp')), may hold values from 0 to 127, all different within a row; in each aligned block of 16 rows (0 to 15, 16 to 31, ...) at most 2 rows name the same one
- route_gates: bfloat16 [8192, 8], P(('expert', 'dp')), may hold values from 0.019897461 to 0.5
- gate_up: bfloat16 [128, 2048, 1536], P('expert', 'dp'), may hold values from -0.125 to 0.125
- down: bfloat16 [128, 2048, 768], P('expert', 'dp'), may hold values from -6 to 6
- moment1: bfloat16 [128, 2048, 768], P('expert', 'dp'), may hold values from -4 to 4
- moment2: bfloat16 [128, 2048, 768], P('expert', 'dp'), may hold values from 0.049804688 to 0.5
- placement: int32 [128], replicated, may hold values from 0 to 127, each once
Outputs:
- rollout_down: bfloat16 [128, 2048, 768], P('expert', None, 'dp')
The draws below stay inside these ranges and needn't reach their ends.
Inputs may be any that keep to these rules, and one draw needn't show every extreme that they name: `route_ids`: each row names 8 different experts; within the rows of one device no expert is named more than 2 times, a bound that some block reaches. `placement`: each expert exactly once.
All inputs are finite; a program needn't handle non-finite values.
Results may differ from the reference program's by a relative error of at most 0.003.
Values may be sent and summed in bfloat16 or wider, within the bound.
A program may use at most 64 MiB of HBM per device.

```python
import math
import jax
import jax.numpy as jnp
import numpy as np
from jax import lax

D = 2048
H = 768
TOP = 8
OPT_STEP = 2
TOK_DEV = 16
EXPERTS = 128
CAP = 2
TOKENS = 8192
N_EXPERT = 128
N_DP = 4


def shard_levels(stream_key, extent, pieces, least, high):
    def one(dim, parts):
        heights = jax.random.uniform(jax.random.fold_in(jax.random.fold_in(stream_key, 6), dim), (parts,), jnp.float32, least / len(pieces), high / len(pieces))
        return jnp.repeat(jnp.exp(heights), extent[dim] // parts).reshape((-1,) + (1,) * (len(extent) - dim - 1))

    loudness = one(*pieces[0])
    for cut in pieces[1:]:
        loudness = loudness * one(*cut)
    return loudness


def routed_block(stream_key, own, number, rows, amount, top, bound, lean):
    sequence = jax.random.permutation(stream_key, amount)
    packed, common = portions_of(amount, rows * top, bound, lean, True), portions_of(amount, rows * top, bound, lean, False)
    places = jnp.arange(amount)

    def named(tallies, offset_by):
        used = int((tallies > 0).sum())
        fixed = max(1, used // 4)
        shifted = fixed + (places - fixed + offset_by * (used - fixed)) % max(1, amount - fixed)
        return jnp.zeros((amount,), jnp.int32).at[sequence[jnp.where(places < fixed, places, shifted)]].set(jnp.asarray(tallies, jnp.int32))

    tallies = jnp.where(number % 4 == 0, named(packed, number // 4), named(common, number - number // 4 - 1))
    mixed = jax.random.permutation(jax.random.fold_in(own, 3), amount)
    source_of, taker = mixed[0:amount // 2 * 2:2], mixed[1:amount // 2 * 2:2]
    slack = jnp.minimum(tallies[source_of] - 1, bound - tallies[taker]) // 2
    slack = jnp.where((source_of == sequence[0]) | (taker == sequence[0]) | (tallies[taker] == 0), 0, jnp.maximum(slack, 0))
    shifted = jax.random.randint(jax.random.fold_in(own, 4), (amount // 2,), 0, 1 << 20) % (slack + 1)
    tallies = tallies.at[source_of].add(-shifted).at[taker].add(shifted)
    labels = jnp.searchsorted(jnp.cumsum(tallies), jnp.arange(rows * top), side="right").astype(jnp.int32)
    listing = labels.reshape(top, rows).T
    listing = listing[jax.random.permutation(jax.random.fold_in(own, 1), rows)]
    offset_by = jax.random.randint(jax.random.fold_in(own, 2), (rows, 1), 0, top)
    return jnp.take_along_axis(listing, (jnp.arange(top)[None, :] + offset_by) % top, axis=1)


def portions_of(count, total, most, skew, full):
    loads = [(1 << 20) // math.isqrt(standing ** skew) + 1 for standing in range(1, count + 1)]
    largest = most if full else min(most, max(-(-total // count), total * loads[0] // sum(loads)))
    least = 1 if total - largest >= count - 1 else 0
    given, spare = [largest] + [least] * (count - 1), total - largest - least * (count - 1)
    while spare > 0:
        free = [i for i in range(1, count) if given[i] < largest] or [i for i in range(1, count) if given[i] < most]
        pool, remaining = sum([loads[i] for i in free]), spare
        for i in free:
            extra = min(most - given[i], max(1, remaining * loads[i] // pool), spare)
            given[i] = given[i] + extra
            spare = spare - extra
    return np.array(given)


def gaussian(stream_key, extent, spread, reach, cuts=(), kind=jnp.bfloat16):
    result = jax.random.normal(stream_key, extent, jnp.float32) * spread
    if len(cuts) > 0:
        result = shard_levels(stream_key, extent, cuts, -0.22, 0.18) * result
    return jnp.clip(result, min=-reach, max=reach).astype(kind)


def setup_inputs(seed: int = 0) -> dict:
    seeds = jax.random.split(jax.random.key(seed), 10)
    tokens = gaussian(seeds[0], (TOKENS, D), 1.0, 6.0, ((0, 512),))
    cotangent = gaussian(seeds[1], (TOKENS, D), 1.0, 6.0, ((0, 512),))
    route_ids_keys = jax.random.split(jax.random.fold_in(seeds[2], 1), TOKENS // TOK_DEV)
    route_ids_turns = jax.random.permutation(jax.random.fold_in(seeds[2], 3), TOKENS // TOK_DEV)
    route_ids = jax.vmap(lambda own, number: routed_block(jax.random.fold_in(seeds[2], 2), own, number, TOK_DEV, EXPERTS, TOP, CAP, 2))(route_ids_keys, route_ids_turns).reshape((TOKENS, TOP))
    route_gates = jnp.clip(jnp.exp(math.log(0.5) - 3.224016 * jax.random.uniform(seeds[3], (TOKENS, TOP), jnp.float32) ** shard_levels(seeds[3], (TOKENS, TOP), ((0, 512),), -0.2, 0.2)), 0.019897461, 0.5).astype(jnp.bfloat16)
    gate_up = gaussian(seeds[4], (EXPERTS, D, 2 * H), D ** -0.5, 0.125, ((0, 128), (1, 4)))
    down = gaussian(seeds[5], (EXPERTS, D, H), 1.0, 6.0, ((0, 128), (1, 4)))
    moment1 = gaussian(seeds[6], (EXPERTS, D, H), 0.3, 4.0, ((0, 128), (1, 4)))
    moment2 = jnp.clip(jnp.exp(math.log(0.5) - 2.306499 * jax.random.uniform(seeds[7], (EXPERTS, D, H), jnp.float32) ** shard_levels(seeds[7], (EXPERTS, D, H), ((0, 128), (1, 4)), -0.2, 0.2)), 0.049804688, 0.5).astype(jnp.bfloat16)
    placement = jax.random.permutation(seeds[8], EXPERTS).astype(jnp.int32)
    return {"tokens": tokens, "cotangent": cotangent, "route_ids": route_ids, "route_gates": route_gates, "gate_up": gate_up, "down": down, "moment1": moment1, "moment2": moment2, "placement": placement}


BETA_ONE = 0.9
BETA_TWO = 0.95
ADAM_EPS = 1e-08
LEARN_RATE = 0.25

def reference(tokens, cotangent, route_ids, route_gates, gate_up, down, moment1, moment2, placement):
    blocks = N_EXPERT * N_DP
    route_table = route_ids.reshape(blocks, TOK_DEV, TOP)
    route_hits = lax.optimization_barrier(jnp.sum((route_table[:, :, :, None] == jnp.arange(EXPERTS, dtype=jnp.int32)).astype(jnp.int32), axis=2))
    earlier_hits = jnp.cumsum(route_hits, axis=1) - route_hits
    slot_index = jnp.take_along_axis(earlier_hits, route_table, axis=2).astype(jnp.int32)
    row_ids = jnp.broadcast_to(jnp.arange(TOKENS, dtype=jnp.int32).reshape(blocks, TOK_DEV, 1), route_table.shape)
    owner_block = jnp.broadcast_to(jnp.arange(blocks, dtype=jnp.int32).reshape(blocks, 1, 1), route_table.shape)
    slot_rows = jnp.full((EXPERTS, blocks, CAP), TOKENS, jnp.int32).at[route_table, owner_block, slot_index].set(row_ids)
    slot_gates = jnp.zeros((EXPERTS, blocks, CAP), jnp.float32).at[route_table, owner_block, slot_index].set(route_gates.reshape(blocks, TOK_DEV, TOP).astype(jnp.float32))
    slot_rows = slot_rows.reshape(EXPERTS, N_EXPERT, N_DP, CAP).transpose(0, 2, 1, 3).reshape(EXPERTS, N_DP, N_EXPERT * CAP)
    slot_gates = slot_gates.reshape(EXPERTS, N_EXPERT, N_DP, CAP).transpose(0, 2, 1, 3).reshape(EXPERTS, N_DP, N_EXPERT * CAP)
    padded_rows = jnp.concatenate([tokens, jnp.zeros((1, D), tokens.dtype)], axis=0)
    padded_grads = jnp.concatenate([cotangent, jnp.zeros((1, D), cotangent.dtype)], axis=0)
    correct_one = 1.0 - BETA_ONE ** OPT_STEP
    correct_two = 1.0 - BETA_TWO ** OPT_STEP

    def per_expert(inputs):
        rows_e, gates_e, weights_e, down_e, first_e, second_e = inputs

        def per_group(running, group_data):
            rows_g, gates_g = group_data
            gathered = padded_rows[rows_g]
            pre = jnp.dot(gathered, weights_e, preferred_element_type=jnp.float32)
            hidden = (jax.nn.silu(pre[:, :H]) * pre[:, H:]).astype(jnp.bfloat16)
            scaled = (gates_g[:, None] * padded_grads[rows_g].astype(jnp.float32)).astype(jnp.bfloat16)
            partial_value = jnp.dot(scaled.T, hidden, preferred_element_type=jnp.float32)
            partial_value = lax.optimization_barrier(partial_value.astype(jnp.bfloat16)).astype(jnp.float32)
            return (running + partial_value, None)
        grad_sum, _ = lax.scan(per_group, jnp.zeros((D, H), jnp.float32), (rows_e, gates_e))
        first = BETA_ONE * first_e.astype(jnp.float32) + (1.0 - BETA_ONE) * grad_sum
        second = BETA_TWO * second_e.astype(jnp.float32) + (1.0 - BETA_TWO) * grad_sum * grad_sum
        direction = first / correct_one / (jnp.sqrt(second / correct_two) + ADAM_EPS)
        updated = down_e.astype(jnp.float32) - LEARN_RATE * direction
        return updated.astype(jnp.bfloat16)
    updated_all = lax.map(per_expert, (slot_rows, slot_gates, gate_up, down, moment1, moment2))
    return jnp.take(updated_all, placement, axis=0)
```

```python
import jax
import jax.numpy as jnp
from jax import lax
from jax.sharding import Mesh, PartitionSpec as P

OPT_STEP = 2


BETA_ONE = 0.9
BETA_TWO = 0.95
ADAM_EPS = 1e-08
LEARN_RATE = 0.25

DP = ("zh", "core")
PLANE = ("x", "y")
EXPERT = ("x", "zl", "y")
CAP = 2
META = 128

contract_rows = (((0,), (0,)), ((), ()))


def pickers(meta, blocks, block_rows, top):
    plane = lax.axis_size(PLANE)
    wide = meta.shape[0]
    ids = meta[:, :top].astype(jnp.int32)
    gates = meta[:, top : 2 * top].astype(jnp.float32)
    place = jnp.arange(plane, dtype=jnp.int32)
    y_size = lax.axis_size("y")
    wanted = (place // y_size * lax.axis_size("zl") + lax.axis_index("zl")) * y_size + place % y_size
    match = (ids[:, :, None] == wanted).astype(jnp.float32)
    hits = jnp.sum(match, axis=1)
    worth = jnp.sum(match * gates[:, :, None], axis=1)
    token = jnp.arange(wide, dtype=jnp.int32)
    own_block = token // block_rows
    before = ((own_block[:, None] == own_block[None, :]) & (token[None, :] < token[:, None])).astype(jnp.bfloat16)
    earlier = jnp.dot(before, hits.astype(jnp.bfloat16), preferred_element_type=jnp.float32)
    row = jnp.arange(plane * blocks * CAP, dtype=jnp.int32)
    row_place = row // (blocks * CAP)
    spread = (row_place[:, None] == place[None, :]).astype(jnp.bfloat16)
    take = lambda v: lax.dot_general(
        spread, v.astype(jnp.bfloat16), (((1,), (1,)), ((), ())), preferred_element_type=jnp.float32
    )
    here = (row // CAP % blocks)[:, None] == own_block[None, :]
    slot = jnp.where(hits > 0, earlier, -1.0)
    chosen = here & (take(slot) == (row % CAP)[:, None].astype(jnp.float32))
    one_hot = chosen.astype(jnp.bfloat16)
    return one_hot, jnp.where(chosen, take(worth), 0.0).astype(jnp.bfloat16)


def shards(tokens, cotangent, route_ids, route_gates, gate_up, down, moment1, moment2, placement):
    tok_rows, width = tokens.shape
    top = route_ids.shape[1]
    hidden_units = down.shape[2]
    groups = lax.axis_size(DP)
    line = lax.axis_size("zl")
    plane = lax.axis_size(PLANE)
    experts = lax.axis_size(EXPERT)
    share = width // groups
    bf16 = jnp.bfloat16

    meta = jnp.concatenate(
        [route_ids.astype(bf16), route_gates, jnp.zeros((tok_rows, META - 2 * top), bf16)], axis=1
    )
    tok_pack = lax.all_gather(jnp.concatenate([tokens, meta], axis=1), "zl", axis=0, tiled=True)

    cot_parts = cotangent.reshape(tok_rows, groups, share).transpose(1, 0, 2)
    cot_parts = jnp.concatenate(
        [cot_parts, jnp.broadcast_to(meta[None], (groups, tok_rows, META))], axis=2
    )
    cot_parts = lax.all_to_all(cot_parts, DP, split_axis=0, concat_axis=0, tiled=True)
    cot_pack = lax.all_gather(
        cot_parts.reshape(groups * tok_rows, share + META), "zl", axis=0, tiled=True
    )

    gate_up, cot_pack, tok_pack = lax.optimization_barrier((gate_up, cot_pack, tok_pack))
    weights = lax.all_gather(gate_up[0], DP, axis=0, tiled=True)

    tok_pick, _ = pickers(tok_pack[:, width:], line, tok_rows, top)
    rows = jnp.dot(tok_pick, tok_pack[:, :width], preferred_element_type=jnp.float32).astype(bf16)
    rows = lax.all_to_all(
        rows.reshape(plane, line * CAP, width), PLANE, split_axis=0, concat_axis=0, tiled=True
    ).reshape(plane * line * CAP, width)

    _, cot_pick = pickers(cot_pack[:, share:], line * groups, tok_rows, top)
    scaled = jnp.dot(cot_pick, cot_pack[:, :share], preferred_element_type=jnp.float32).astype(bf16)
    scaled = lax.all_to_all(
        scaled.reshape(plane, line * groups * CAP, share), PLANE, split_axis=0, concat_axis=0, tiled=True
    )
    scaled = scaled.reshape(plane * line, groups, CAP, share).transpose(1, 0, 2, 3)
    scaled = scaled.reshape(groups * plane * line * CAP, share)

    pre = jnp.dot(rows, weights, preferred_element_type=jnp.float32)
    hidden = (jax.nn.silu(pre[:, :hidden_units]) * pre[:, hidden_units:]).astype(bf16)
    hidden = lax.all_gather(hidden, DP, axis=0, tiled=True)
    grad = lax.dot_general(scaled, hidden, contract_rows, preferred_element_type=jnp.float32)

    correct_one = 1.0 - BETA_ONE**OPT_STEP
    correct_two = 1.0 - BETA_TWO**OPT_STEP
    first = BETA_ONE * moment1[0].astype(jnp.float32) + (1.0 - BETA_ONE) * grad
    second = BETA_TWO * moment2[0].astype(jnp.float32) + (1.0 - BETA_TWO) * grad * grad
    direction = first / correct_one / (jnp.sqrt(second / correct_two) + ADAM_EPS)
    updated = (down[0].astype(jnp.float32) - LEARN_RATE * direction).astype(bf16)

    block_cols = hidden_units // groups
    piece_rows = share // experts
    pieces = updated.reshape(experts, piece_rows, groups, block_cols).transpose(0, 2, 1, 3)
    pieces = pieces.reshape(experts * groups, piece_rows * block_cols)
    spread = lax.all_to_all(pieces, EXPERT + DP, split_axis=0, concat_axis=0, tiled=True)
    spread = spread.reshape(experts, groups * piece_rows * block_cols)
    picked = jnp.take(spread, placement, axis=0)
    landed = lax.all_to_all(picked, EXPERT, split_axis=0, concat_axis=0, tiled=True)
    landed = landed.reshape(experts, groups, piece_rows, block_cols).transpose(1, 0, 2, 3)
    return landed.reshape(1, width, block_cols)


def solution(mesh):
    grid = Mesh(mesh.devices.reshape(4, 8, 4, 2, 2), EXPERT + DP)
    every = P(EXPERT + DP, None)
    owned = P(EXPERT, DP, None)
    placed = (every, every, every, every, owned, owned, owned, owned, P())
    return jax.shard_map(
        shards, mesh=grid, in_specs=placed, out_specs=P(EXPERT, None, DP), check_vma=False
    )
```

```python
import jax
import jax.numpy as jnp
from jax import lax
from jax.sharding import Mesh, PartitionSpec as P

OPT_STEP = 2


BETA_ONE = 0.9
BETA_TWO = 0.95
ADAM_EPS = 1e-08
LEARN_RATE = 0.25

DP = ("zh", "core")
PLANE = ("x", "y")
EXPERT = ("x", "zl", "y")
CAP = 2
META = 128

contract_rows = (((0,), (0,)), ((), ()))


def pickers(meta, blocks, block_rows, top):
    plane = lax.axis_size(PLANE)
    wide = meta.shape[0]
    ids = meta[:, :top].astype(jnp.int32)
    gates = meta[:, top : 2 * top].astype(jnp.float32)
    place = jnp.arange(plane, dtype=jnp.int32)
    y_size = lax.axis_size("y")
    wanted = (place // y_size * lax.axis_size("zl") + lax.axis_index("zl")) * y_size + place % y_size
    match = (ids[:, :, None] == wanted).astype(jnp.float32)
    hits = jnp.sum(match, axis=1)
    worth = jnp.sum(match * gates[:, :, None], axis=1)
    token = jnp.arange(wide, dtype=jnp.int32)
    own_block = token // block_rows
    before = ((own_block[:, None] == own_block[None, :]) & (token[None, :] < token[:, None])).astype(jnp.bfloat16)
    earlier = jnp.dot(before, hits.astype(jnp.bfloat16), preferred_element_type=jnp.float32)
    row = jnp.arange(plane * blocks * CAP, dtype=jnp.int32)
    row_place = row // (blocks * CAP)
    spread = (row_place[:, None] == place[None, :]).astype(jnp.bfloat16)
    take = lambda v: lax.dot_general(
        spread, v.astype(jnp.bfloat16), (((1,), (1,)), ((), ())), preferred_element_type=jnp.float32
    )
    here = (row // CAP % blocks)[:, None] == own_block[None, :]
    slot = jnp.where(hits > 0, earlier, -1.0)
    chosen = here & (take(slot) == (row % CAP)[:, None].astype(jnp.float32))
    one_hot = chosen.astype(jnp.bfloat16)
    return one_hot, jnp.where(chosen, take(worth), 0.0).astype(jnp.bfloat16)


def shards(tokens, cotangent, route_ids, route_gates, gate_up, down, moment1, moment2, placement):
    tok_rows, width = tokens.shape
    top = route_ids.shape[1]
    hidden_units = down.shape[2]
    groups = lax.axis_size(DP)
    line = lax.axis_size("zl")
    plane = lax.axis_size(PLANE)
    experts = lax.axis_size(EXPERT)
    share = width // groups
    bf16 = jnp.bfloat16

    meta = jnp.concatenate(
        [route_ids.astype(bf16), route_gates, jnp.zeros((tok_rows, META - 2 * top), bf16)], axis=1
    )
    tok_pack = lax.all_gather(jnp.concatenate([tokens, meta], axis=1), "zl", axis=0, tiled=True)

    cot_parts = cotangent.reshape(tok_rows, groups, share).transpose(1, 0, 2)
    cot_parts = jnp.concatenate(
        [cot_parts, jnp.broadcast_to(meta[None], (groups, tok_rows, META))], axis=2
    )
    cot_parts = lax.all_to_all(cot_parts, DP, split_axis=0, concat_axis=0, tiled=True)
    cot_pack = lax.all_gather(
        cot_parts.reshape(groups * tok_rows, share + META), "zl", axis=0, tiled=True
    )

    weights = lax.all_gather(gate_up[0], DP, axis=0, tiled=True)

    tok_pick, _ = pickers(tok_pack[:, width:], line, tok_rows, top)
    rows = jnp.dot(tok_pick, tok_pack[:, :width], preferred_element_type=jnp.float32).astype(bf16)
    rows = lax.all_to_all(
        rows.reshape(plane, line * CAP, width), PLANE, split_axis=0, concat_axis=0, tiled=True
    ).reshape(plane * line * CAP, width)

    _, cot_pick = pickers(cot_pack[:, share:], line * groups, tok_rows, top)
    scaled = jnp.dot(cot_pick, cot_pack[:, :share], preferred_element_type=jnp.float32).astype(bf16)
    scaled = lax.all_to_all(
        scaled.reshape(plane, line * groups * CAP, share), PLANE, split_axis=0, concat_axis=0, tiled=True
    )
    scaled = scaled.reshape(plane * line, groups, CAP, share).transpose(1, 0, 2, 3)
    scaled = scaled.reshape(groups * plane * line * CAP, share)

    pre = jnp.dot(rows, weights, preferred_element_type=jnp.float32)
    hidden = (jax.nn.silu(pre[:, :hidden_units]) * pre[:, hidden_units:]).astype(bf16)
    hidden = lax.all_gather(hidden, DP, axis=0, tiled=True)
    grad = lax.dot_general(scaled, hidden, contract_rows, preferred_element_type=jnp.float32)

    correct_one = 1.0 - BETA_ONE**OPT_STEP
    correct_two = 1.0 - BETA_TWO**OPT_STEP
    first = BETA_ONE * moment1[0].astype(jnp.float32) + (1.0 - BETA_ONE) * grad
    second = BETA_TWO * moment2[0].astype(jnp.float32) + (1.0 - BETA_TWO) * grad * grad
    direction = first / correct_one / (jnp.sqrt(second / correct_two) + ADAM_EPS)
    updated = (down[0].astype(jnp.float32) - LEARN_RATE * direction).astype(bf16)

    block_cols = hidden_units // groups
    piece_rows = share // experts
    pieces = updated.reshape(experts, piece_rows, groups, block_cols).transpose(0, 2, 1, 3)
    pieces = pieces.reshape(experts * groups, piece_rows * block_cols)
    spread = lax.all_to_all(pieces, EXPERT + DP, split_axis=0, concat_axis=0, tiled=True)
    spread = spread.reshape(experts, groups * piece_rows * block_cols)
    picked = jnp.take(spread, placement, axis=0)
    landed = lax.all_to_all(picked, EXPERT, split_axis=0, concat_axis=0, tiled=True)
    landed = landed.reshape(experts, groups, piece_rows, block_cols).transpose(1, 0, 2, 3)
    return landed.reshape(1, width, block_cols)


def solution(mesh):
    grid = Mesh(mesh.devices.reshape(4, 8, 4, 2, 2), EXPERT + DP)
    every = P(EXPERT + DP, None)
    owned = P(EXPERT, DP, None)
    placed = (every, every, every, every, owned, owned, owned, owned, P())
    return jax.shard_map(
        shards, mesh=grid, in_specs=placed, out_specs=P(EXPERT, None, DP), check_vma=False
    )
```

```python
import jax
import jax.numpy as jnp
from jax import lax
from jax.experimental import pallas as pl
from jax.experimental.pallas import tpu as pltpu
from jax.sharding import Mesh, PartitionSpec as P

OPT_STEP = 2


BETA_ONE = 0.9
BETA_TWO = 0.95
ADAM_EPS = 1e-08
LEARN_RATE = 0.25

DP = ("zh", "core")
PLANE = ("x", "y")
EXPERT = ("x", "zl", "y")
CAP = 2
META = 128

contract_rows = (((0,), (0,)), ((), ()))


LINE = 8
MESH = pl.DeviceIdType.MESH


def line_gather_kernel(
    tok_ref, cot_ref, tok_all, cot_all, tok_recv, tok_send, cot_recv, cot_send, dp_recv, dp_send, own_sem
):
    at, zh, core = lax.axis_index("zl"), lax.axis_index("zh"), lax.axis_index("core")
    me = zh * 2 + core
    has = (at < LINE - 1, at > 0)
    ids = ({"zl": jnp.minimum(at + 1, LINE - 1)}, {"zl": jnp.maximum(at - 1, 0)})
    partners = []
    for dz, dc in ((0, 1), (1, 0), (1, 1)):
        partners.append(((zh + dz) % 2, (core + dc) % 2))

    barrier = pltpu.get_barrier_semaphore()
    for far in (0, 1):

        @pl.when(has[far])
        def _():
            pl.semaphore_signal(barrier, inc=1, device_id=ids[far], device_id_type=MESH)

    for pz, pc in partners:
        pl.semaphore_signal(barrier, inc=1, device_id={"zh": pz, "core": pc}, device_id_type=MESH)
    pl.semaphore_wait(barrier, 3 + has[0].astype(jnp.int32) + has[1].astype(jnp.int32))

    def hop(out, recv, send, block, far, source=None):
        return pltpu.make_async_remote_copy(
            src_ref=out.at[block] if source is None else source,
            dst_ref=out.at[block],
            send_sem=send.at[far, block],
            recv_sem=recv.at[block],
            device_id=ids[far],
            device_id_type=MESH,
        )

    def first(out, recv, send, source=None):
        for far in (0, 1):

            @pl.when(has[far])
            def _():
                hop(out, recv, send, at, far, source).start()

    def step(out, recv, send, s):
        for far in (0, 1):
            block = at - s if far == 0 else at + s
            there = block >= 0 if far == 0 else block < LINE

            @pl.when(there)
            def _():
                hop(out, recv, send, block, far).wait_recv()

            @pl.when(there & has[far])
            def _():
                hop(out, recv, send, block, far).start()

    def finish(out, recv, send, source=None):
        for s in range(LINE):
            for far in (0, 1):
                block = at - s if far == 0 else at + s
                there = block >= 0 if far == 0 else block < LINE

                @pl.when(there & has[far])
                def _():
                    hop(out, recv, send, block, far, source if s == 0 else None).wait_send()

    own_tok = pltpu.make_async_copy(tok_ref, tok_all.at[at], own_sem.at[0])
    own_cot = pltpu.make_async_copy(cot_ref.at[me], cot_all.at[at, me], own_sem.at[1])
    swaps = [
        pltpu.make_async_remote_copy(
            src_ref=cot_ref.at[pz * 2 + pc],
            dst_ref=cot_all.at[at, me],
            send_sem=dp_send.at[k],
            recv_sem=dp_recv.at[k],
            device_id={"zh": pz, "core": pc},
            device_id_type=MESH,
        )
        for k, (pz, pc) in enumerate(partners)
    ]
    tok = (tok_all, tok_recv, tok_send)
    cot = (cot_all, cot_recv, cot_send)
    for swap in swaps:
        swap.start()
    first(*tok, tok_ref)
    own_tok.start()
    own_cot.start()
    lead = 3
    for s in range(1, lead):
        step(*tok, s)
    for swap in swaps:
        swap.wait()
    own_cot.wait()
    first(*cot)
    for s in range(lead, LINE + lead - 1):
        if s < LINE:
            step(*tok, s)
        step(*cot, s - lead + 1)
    own_tok.wait()
    finish(*tok, tok_ref)
    finish(*cot)


def line_gather(tok, cot):
    dma = pltpu.SemaphoreType.DMA
    return pl.pallas_call(
        line_gather_kernel,
        out_shape=(
            jax.ShapeDtypeStruct((LINE,) + tok.shape, tok.dtype),
            jax.ShapeDtypeStruct((LINE,) + cot.shape, cot.dtype),
        ),
        in_specs=[pl.BlockSpec(memory_space=pltpu.VMEM)] * 2,
        out_specs=(pl.BlockSpec(memory_space=pltpu.VMEM),) * 2,
        scratch_shapes=[
            dma((LINE,)),
            dma((2, LINE)),
            dma((LINE,)),
            dma((2, LINE)),
            dma((3,)),
            dma((3,)),
            dma((2,)),
        ],
        compiler_params=pltpu.CompilerParams(collective_id=0, has_side_effects=True),
    )(tok, cot)


def pickers(meta, blocks, block_rows, top):
    plane = lax.axis_size(PLANE)
    wide = meta.shape[0]
    ids = meta[:, :top].astype(jnp.int32)
    gates = meta[:, top : 2 * top].astype(jnp.float32)
    place = jnp.arange(plane, dtype=jnp.int32)
    y_size = lax.axis_size("y")
    wanted = (place // y_size * lax.axis_size("zl") + lax.axis_index("zl")) * y_size + place % y_size
    match = (ids[:, :, None] == wanted).astype(jnp.float32)
    hits = jnp.sum(match, axis=1)
    worth = jnp.sum(match * gates[:, :, None], axis=1)
    token = jnp.arange(wide, dtype=jnp.int32)
    own_block = token // block_rows
    before = ((own_block[:, None] == own_block[None, :]) & (token[None, :] < token[:, None])).astype(jnp.bfloat16)
    earlier = jnp.dot(before, hits.astype(jnp.bfloat16), preferred_element_type=jnp.float32)
    row = jnp.arange(plane * blocks * CAP, dtype=jnp.int32)
    row_place = row // (blocks * CAP)
    spread = (row_place[:, None] == place[None, :]).astype(jnp.bfloat16)
    take = lambda v: lax.dot_general(
        spread, v.astype(jnp.bfloat16), (((1,), (1,)), ((), ())), preferred_element_type=jnp.float32
    )
    here = (row // CAP % blocks)[:, None] == own_block[None, :]
    slot = jnp.where(hits > 0, earlier, -1.0)
    chosen = here & (take(slot) == (row % CAP)[:, None].astype(jnp.float32))
    one_hot = chosen.astype(jnp.bfloat16)
    return one_hot, jnp.where(chosen, take(worth), 0.0).astype(jnp.bfloat16)


def shards(tokens, cotangent, route_ids, route_gates, gate_up, down, moment1, moment2, placement):
    tok_rows, width = tokens.shape
    top = route_ids.shape[1]
    hidden_units = down.shape[2]
    groups = lax.axis_size(DP)
    line = lax.axis_size("zl")
    plane = lax.axis_size(PLANE)
    experts = lax.axis_size(EXPERT)
    share = width // groups
    bf16 = jnp.bfloat16

    meta = jnp.concatenate(
        [route_ids.astype(bf16), route_gates, jnp.zeros((tok_rows, META - 2 * top), bf16)], axis=1
    )
    cot_parts = cotangent.reshape(tok_rows, groups, share).transpose(1, 0, 2)
    cot_parts = jnp.concatenate(
        [cot_parts, jnp.broadcast_to(meta[None], (groups, tok_rows, META))], axis=2
    )
    tok_line, cot_line = line_gather(tokens, cot_parts)
    gate_up, tok_line, cot_line = lax.optimization_barrier((gate_up, tok_line, cot_line))
    tok_line = tok_line.reshape(line * tok_rows, width)
    own_meta = lax.dynamic_index_in_dim(cot_line[:, :, :, share:], lax.axis_index(DP), 1, keepdims=False)
    own_meta = own_meta.reshape(line * tok_rows, META)
    cot_pack = cot_line.reshape(line * groups * tok_rows, share + META)
    weights = lax.all_gather(gate_up[0], DP, axis=0, tiled=True)

    tok_pick, _ = pickers(own_meta, line, tok_rows, top)
    rows = jnp.dot(tok_pick, tok_line, preferred_element_type=jnp.float32).astype(bf16)
    rows = lax.all_to_all(
        rows.reshape(plane, line * CAP, width), PLANE, split_axis=0, concat_axis=0, tiled=True
    ).reshape(plane * line * CAP, width)

    _, cot_pick = pickers(cot_pack[:, share:], line * groups, tok_rows, top)
    scaled = jnp.dot(cot_pick, cot_pack[:, :share], preferred_element_type=jnp.float32).astype(bf16)
    scaled = lax.all_to_all(
        scaled.reshape(plane, line * groups * CAP, share), PLANE, split_axis=0, concat_axis=0, tiled=True
    )
    scaled = scaled.reshape(plane * line, groups, CAP, share).transpose(1, 0, 2, 3)
    scaled = scaled.reshape(groups * plane * line * CAP, share)

    weights, scaled = lax.optimization_barrier((weights, scaled))
    pre = jnp.dot(rows, weights, preferred_element_type=jnp.float32)
    hidden = (jax.nn.silu(pre[:, :hidden_units]) * pre[:, hidden_units:]).astype(bf16)
    hidden = lax.all_gather(hidden, DP, axis=0, tiled=True)
    grad = lax.dot_general(scaled, hidden, contract_rows, preferred_element_type=jnp.float32)

    correct_one = 1.0 - BETA_ONE**OPT_STEP
    correct_two = 1.0 - BETA_TWO**OPT_STEP
    first = BETA_ONE * moment1[0].astype(jnp.float32) + (1.0 - BETA_ONE) * grad
    second = BETA_TWO * moment2[0].astype(jnp.float32) + (1.0 - BETA_TWO) * grad * grad
    direction = first / correct_one / (jnp.sqrt(second / correct_two) + ADAM_EPS)
    updated = (down[0].astype(jnp.float32) - LEARN_RATE * direction).astype(bf16)

    block_cols = hidden_units // groups
    piece_rows = share // experts
    pieces = updated.reshape(experts, piece_rows, groups, block_cols).transpose(0, 2, 1, 3)
    pieces = pieces.reshape(experts * groups, piece_rows * block_cols)
    spread = lax.all_to_all(pieces, EXPERT + DP, split_axis=0, concat_axis=0, tiled=True)
    spread = spread.reshape(experts, groups * piece_rows * block_cols)
    picked = jnp.take(spread, placement, axis=0)
    landed = lax.all_to_all(picked, EXPERT, split_axis=0, concat_axis=0, tiled=True)
    landed = landed.reshape(experts, groups, piece_rows, block_cols).transpose(1, 0, 2, 3)
    return landed.reshape(1, width, block_cols)


def solution(mesh):
    grid = Mesh(mesh.devices.reshape(4, 8, 4, 2, 2), EXPERT + DP)
    every = P(EXPERT + DP, None)
    owned = P(EXPERT, DP, None)
    placed = (every, every, every, every, owned, owned, owned, owned, P())
    return jax.shard_map(
        shards, mesh=grid, in_specs=placed, out_specs=P(EXPERT, None, DP), check_vma=False
    )
```

```python
import jax
import jax.numpy as jnp
from jax import lax
from jax.experimental import pallas as pl
from jax.experimental.pallas import tpu as pltpu
from jax.sharding import Mesh, PartitionSpec as P

OPT_STEP = 2


BETA_ONE = 0.9
BETA_TWO = 0.95
ADAM_EPS = 1e-08
LEARN_RATE = 0.25

DP = ("zh", "core")
PLANE = ("x", "y")
EXPERT = ("x", "zl", "y")
CAP = 2
META = 128

contract_rows = (((0,), (0,)), ((), ()))


LINE = 8
MESH = pl.DeviceIdType.MESH


def line_gather_kernel(
    tok_ref, cot_ref, tok_all, cot_all, tok_recv, tok_send, cot_recv, cot_send, dp_recv, dp_send, own_sem
):
    at, zh, core = lax.axis_index("zl"), lax.axis_index("zh"), lax.axis_index("core")
    me = zh * 2 + core
    has = (at < LINE - 1, at > 0)
    ids = ({"zl": jnp.minimum(at + 1, LINE - 1)}, {"zl": jnp.maximum(at - 1, 0)})
    partners = []
    for dz, dc in ((0, 1), (1, 0), (1, 1)):
        partners.append(((zh + dz) % 2, (core + dc) % 2))

    barrier = pltpu.get_barrier_semaphore()
    for far in (0, 1):

        @pl.when(has[far])
        def _():
            pl.semaphore_signal(barrier, inc=1, device_id=ids[far], device_id_type=MESH)

    for pz, pc in partners:
        pl.semaphore_signal(barrier, inc=1, device_id={"zh": pz, "core": pc}, device_id_type=MESH)
    pl.semaphore_wait(barrier, 3 + has[0].astype(jnp.int32) + has[1].astype(jnp.int32))

    def hop(out, recv, send, block, far, source=None):
        return pltpu.make_async_remote_copy(
            src_ref=out.at[block] if source is None else source,
            dst_ref=out.at[block],
            send_sem=send.at[far, block],
            recv_sem=recv.at[block],
            device_id=ids[far],
            device_id_type=MESH,
        )

    def first(out, recv, send, source=None):
        for far in (0, 1):

            @pl.when(has[far])
            def _():
                hop(out, recv, send, at, far, source).start()

    def step(out, recv, send, s):
        for far in (0, 1):
            block = at - s if far == 0 else at + s
            there = block >= 0 if far == 0 else block < LINE

            @pl.when(there)
            def _():
                hop(out, recv, send, block, far).wait_recv()

            @pl.when(there & has[far])
            def _():
                hop(out, recv, send, block, far).start()

    def finish(out, recv, send, source=None):
        for s in range(LINE):
            for far in (0, 1):
                block = at - s if far == 0 else at + s
                there = block >= 0 if far == 0 else block < LINE

                @pl.when(there & has[far])
                def _():
                    hop(out, recv, send, block, far, source if s == 0 else None).wait_send()

    own_tok = pltpu.make_async_copy(tok_ref, tok_all.at[at], own_sem.at[0])
    own_cot = pltpu.make_async_copy(cot_ref.at[me], cot_all.at[at, me], own_sem.at[1])
    swaps = [
        pltpu.make_async_remote_copy(
            src_ref=cot_ref.at[pz * 2 + pc],
            dst_ref=cot_all.at[at, me],
            send_sem=dp_send.at[k],
            recv_sem=dp_recv.at[k],
            device_id={"zh": pz, "core": pc},
            device_id_type=MESH,
        )
        for k, (pz, pc) in enumerate(partners)
    ]
    tok = (tok_all, tok_recv, tok_send)
    cot = (cot_all, cot_recv, cot_send)
    for swap in swaps:
        swap.start()
    first(*tok, tok_ref)
    own_tok.start()
    own_cot.start()
    lead = 3
    for s in range(1, lead):
        step(*tok, s)
    for swap in swaps:
        swap.wait()
    own_cot.wait()
    first(*cot)
    for s in range(lead, LINE + lead - 1):
        if s < LINE:
            step(*tok, s)
        step(*cot, s - lead + 1)
    own_tok.wait()
    finish(*tok, tok_ref)
    finish(*cot)


def line_gather(tok, cot):
    dma = pltpu.SemaphoreType.DMA
    return pl.pallas_call(
        line_gather_kernel,
        out_shape=(
            jax.ShapeDtypeStruct((LINE,) + tok.shape, tok.dtype),
            jax.ShapeDtypeStruct((LINE,) + cot.shape, cot.dtype),
        ),
        in_specs=[pl.BlockSpec(memory_space=pltpu.VMEM)] * 2,
        out_specs=(pl.BlockSpec(memory_space=pltpu.VMEM),) * 2,
        scratch_shapes=[
            dma((LINE,)),
            dma((2, LINE)),
            dma((LINE,)),
            dma((2, LINE)),
            dma((3,)),
            dma((3,)),
            dma((2,)),
        ],
        compiler_params=pltpu.CompilerParams(collective_id=0, has_side_effects=True),
    )(tok, cot)


def pickers(meta, blocks, block_rows, top):
    plane = lax.axis_size(PLANE)
    wide = meta.shape[0]
    ids = meta[:, :top].astype(jnp.int32)
    gates = meta[:, top : 2 * top].astype(jnp.float32)
    place = jnp.arange(plane, dtype=jnp.int32)
    y_size = lax.axis_size("y")
    wanted = (place // y_size * lax.axis_size("zl") + lax.axis_index("zl")) * y_size + place % y_size
    match = (ids[:, :, None] == wanted).astype(jnp.float32)
    hits = jnp.sum(match, axis=1)
    worth = jnp.sum(match * gates[:, :, None], axis=1)
    token = jnp.arange(wide, dtype=jnp.int32)
    own_block = token // block_rows
    before = ((own_block[:, None] == own_block[None, :]) & (token[None, :] < token[:, None])).astype(jnp.bfloat16)
    earlier = jnp.dot(before, hits.astype(jnp.bfloat16), preferred_element_type=jnp.float32)
    row = jnp.arange(plane * blocks * CAP, dtype=jnp.int32)
    row_place = row // (blocks * CAP)
    spread = (row_place[:, None] == place[None, :]).astype(jnp.bfloat16)
    take = lambda v: lax.dot_general(
        spread, v.astype(jnp.bfloat16), (((1,), (1,)), ((), ())), preferred_element_type=jnp.float32
    )
    here = (row // CAP % blocks)[:, None] == own_block[None, :]
    slot = jnp.where(hits > 0, earlier, -1.0)
    chosen = here & (take(slot) == (row % CAP)[:, None].astype(jnp.float32))
    one_hot = chosen.astype(jnp.bfloat16)
    return one_hot, jnp.where(chosen, take(worth), 0.0).astype(jnp.bfloat16)


def shards(tokens, cotangent, route_ids, route_gates, gate_up, down, moment1, moment2, placement):
    tok_rows, width = tokens.shape
    top = route_ids.shape[1]
    hidden_units = down.shape[2]
    groups = lax.axis_size(DP)
    line = lax.axis_size("zl")
    plane = lax.axis_size(PLANE)
    experts = lax.axis_size(EXPERT)
    share = width // groups
    bf16 = jnp.bfloat16

    meta = jnp.concatenate(
        [route_ids.astype(bf16), route_gates, jnp.zeros((tok_rows, META - 2 * top), bf16)], axis=1
    )
    cot_parts = cotangent.reshape(tok_rows, groups, share).transpose(1, 0, 2)
    cot_parts = jnp.concatenate(
        [cot_parts, jnp.broadcast_to(meta[None], (groups, tok_rows, META))], axis=2
    )
    tok_line, cot_line = line_gather(tokens, cot_parts)
    tok_line = tok_line.reshape(line * tok_rows, width)
    own_meta = lax.dynamic_index_in_dim(cot_line[:, :, :, share:], lax.axis_index(DP), 1, keepdims=False)
    own_meta = own_meta.reshape(line * tok_rows, META)
    cot_pack = cot_line.reshape(line * groups * tok_rows, share + META)
    weights = lax.all_gather(gate_up[0], DP, axis=0, tiled=True)

    tok_pick, _ = pickers(own_meta, line, tok_rows, top)
    rows = jnp.dot(tok_pick, tok_line, preferred_element_type=jnp.float32).astype(bf16)
    rows = lax.all_to_all(
        rows.reshape(plane, line * CAP, width), PLANE, split_axis=0, concat_axis=0, tiled=True
    ).reshape(plane * line * CAP, width)

    _, cot_pick = pickers(cot_pack[:, share:], line * groups, tok_rows, top)
    scaled = jnp.dot(cot_pick, cot_pack[:, :share], preferred_element_type=jnp.float32).astype(bf16)
    scaled = lax.all_to_all(
        scaled.reshape(plane, line * groups * CAP, share), PLANE, split_axis=0, concat_axis=0, tiled=True
    )
    scaled = scaled.reshape(plane * line, groups, CAP, share).transpose(1, 0, 2, 3)
    scaled = scaled.reshape(groups * plane * line * CAP, share)

    weights, scaled = lax.optimization_barrier((weights, scaled))
    pre = jnp.dot(rows, weights, preferred_element_type=jnp.float32)
    hidden = (jax.nn.silu(pre[:, :hidden_units]) * pre[:, hidden_units:]).astype(bf16)
    hidden = lax.all_gather(hidden, DP, axis=0, tiled=True)
    grad = lax.dot_general(scaled, hidden, contract_rows, preferred_element_type=jnp.float32)

    correct_one = 1.0 - BETA_ONE**OPT_STEP
    correct_two = 1.0 - BETA_TWO**OPT_STEP
    first = BETA_ONE * moment1[0].astype(jnp.float32) + (1.0 - BETA_ONE) * grad
    second = BETA_TWO * moment2[0].astype(jnp.float32) + (1.0 - BETA_TWO) * grad * grad
    direction = first / correct_one / (jnp.sqrt(second / correct_two) + ADAM_EPS)
    updated = (down[0].astype(jnp.float32) - LEARN_RATE * direction).astype(bf16)

    block_cols = hidden_units // groups
    piece_rows = share // experts
    pieces = updated.reshape(experts, piece_rows, groups, block_cols).transpose(0, 2, 1, 3)
    pieces = pieces.reshape(experts * groups, CAP, piece_rows * block_cols // CAP)
    spread = lax.all_to_all(pieces, EXPERT + DP, split_axis=0, concat_axis=0, tiled=True)
    spread = spread.reshape(experts, CAP, groups * piece_rows * block_cols // CAP)
    picked = jnp.take(spread, placement, axis=0, mode="clip")
    landed = lax.all_to_all(picked, EXPERT, split_axis=0, concat_axis=0, tiled=True)
    landed = landed.reshape(experts, groups, piece_rows, block_cols).transpose(1, 0, 2, 3)
    return landed.reshape(1, width, block_cols)


def solution(mesh):
    grid = Mesh(mesh.devices.reshape(4, 8, 4, 2, 2), EXPERT + DP)
    every = P(EXPERT + DP, None)
    owned = P(EXPERT, DP, None)
    placed = (every, every, every, every, owned, owned, owned, owned, P())
    return jax.shard_map(
        shards, mesh=grid, in_specs=placed, out_specs=P(EXPERT, None, DP), check_vma=False
    )
```

```python
import jax
import jax.numpy as jnp
from jax import lax
from jax.experimental import pallas as pl
from jax.experimental.pallas import tpu as pltpu
from jax.sharding import Mesh, PartitionSpec as P

OPT_STEP = 2


BETA_ONE = 0.9
BETA_TWO = 0.95
ADAM_EPS = 1e-08
LEARN_RATE = 0.25

DP = ("zh", "core")
PLANE = ("x", "y")
EXPERT = ("x", "zl", "y")
CAP = 2
META = 128

contract_rows = (((0,), (0,)), ((), ()))


LINE = 8
MESH = pl.DeviceIdType.MESH


def line_gather_kernel(
    tok_ref, cot_ref, tok_all, cot_all, tok_recv, tok_send, cot_recv, cot_send, dp_recv, dp_send, own_sem
):
    at, zh, core = lax.axis_index("zl"), lax.axis_index("zh"), lax.axis_index("core")
    me = zh * 2 + core
    has = (at < LINE - 1, at > 0)
    ids = ({"zl": jnp.minimum(at + 1, LINE - 1)}, {"zl": jnp.maximum(at - 1, 0)})
    partners = []
    for dz, dc in ((0, 1), (1, 0), (1, 1)):
        partners.append(((zh + dz) % 2, (core + dc) % 2))

    barrier = pltpu.get_barrier_semaphore()
    for far in (0, 1):

        @pl.when(has[far])
        def _():
            pl.semaphore_signal(barrier, inc=1, device_id=ids[far], device_id_type=MESH)

    for pz, pc in partners:
        pl.semaphore_signal(barrier, inc=1, device_id={"zh": pz, "core": pc}, device_id_type=MESH)
    pl.semaphore_wait(barrier, 3 + has[0].astype(jnp.int32) + has[1].astype(jnp.int32))

    def hop(out, recv, send, block, far, source=None):
        return pltpu.make_async_remote_copy(
            src_ref=out.at[block] if source is None else source,
            dst_ref=out.at[block],
            send_sem=send.at[far, block],
            recv_sem=recv.at[block],
            device_id=ids[far],
            device_id_type=MESH,
        )

    def first(out, recv, send, source=None):
        for far in (0, 1):

            @pl.when(has[far])
            def _():
                hop(out, recv, send, at, far, source).start()

    def step(out, recv, send, s):
        for far in (0, 1):
            block = at - s if far == 0 else at + s
            there = block >= 0 if far == 0 else block < LINE

            @pl.when(there)
            def _():
                hop(out, recv, send, block, far).wait_recv()

            @pl.when(there & has[far])
            def _():
                hop(out, recv, send, block, far).start()

    def finish(out, recv, send, source=None):
        for s in range(LINE):
            for far in (0, 1):
                block = at - s if far == 0 else at + s
                there = block >= 0 if far == 0 else block < LINE

                @pl.when(there & has[far])
                def _():
                    hop(out, recv, send, block, far, source if s == 0 else None).wait_send()

    own_tok = pltpu.make_async_copy(tok_ref, tok_all.at[at], own_sem.at[0])
    own_cot = pltpu.make_async_copy(cot_ref.at[me], cot_all.at[at, me], own_sem.at[1])
    swaps = [
        pltpu.make_async_remote_copy(
            src_ref=cot_ref.at[pz * 2 + pc],
            dst_ref=cot_all.at[at, me],
            send_sem=dp_send.at[k],
            recv_sem=dp_recv.at[k],
            device_id={"zh": pz, "core": pc},
            device_id_type=MESH,
        )
        for k, (pz, pc) in enumerate(partners)
    ]
    tok = (tok_all, tok_recv, tok_send)
    cot = (cot_all, cot_recv, cot_send)
    for swap in swaps:
        swap.start()
    first(*tok, tok_ref)
    own_tok.start()
    own_cot.start()
    lead = 3
    for s in range(1, lead):
        step(*tok, s)
    for swap in swaps:
        swap.wait()
    own_cot.wait()
    first(*cot)
    for s in range(lead, LINE + lead - 1):
        if s < LINE:
            step(*tok, s)
        step(*cot, s - lead + 1)
    own_tok.wait()
    finish(*tok, tok_ref)
    finish(*cot)


def line_gather(tok, cot):
    dma = pltpu.SemaphoreType.DMA
    return pl.pallas_call(
        line_gather_kernel,
        out_shape=(
            jax.ShapeDtypeStruct((LINE,) + tok.shape, tok.dtype),
            jax.ShapeDtypeStruct((LINE,) + cot.shape, cot.dtype),
        ),
        in_specs=[pl.BlockSpec(memory_space=pltpu.VMEM)] * 2,
        out_specs=(pl.BlockSpec(memory_space=pltpu.VMEM),) * 2,
        scratch_shapes=[
            dma((LINE,)),
            dma((2, LINE)),
            dma((LINE,)),
            dma((2, LINE)),
            dma((3,)),
            dma((3,)),
            dma((2,)),
        ],
        compiler_params=pltpu.CompilerParams(collective_id=0, has_side_effects=True),
    )(tok, cot)


def pickers(meta, blocks, block_rows, top):
    plane = lax.axis_size(PLANE)
    wide = meta.shape[0]
    ids = meta[:, :top].astype(jnp.int32)
    gates = meta[:, top : 2 * top].astype(jnp.float32)
    place = jnp.arange(plane, dtype=jnp.int32)
    y_size = lax.axis_size("y")
    wanted = (place // y_size * lax.axis_size("zl") + lax.axis_index("zl")) * y_size + place % y_size
    match = (ids[:, :, None] == wanted).astype(jnp.float32)
    hits = jnp.sum(match, axis=1)
    worth = jnp.sum(match * gates[:, :, None], axis=1)
    token = jnp.arange(wide, dtype=jnp.int32)
    own_block = token // block_rows
    before = ((own_block[:, None] == own_block[None, :]) & (token[None, :] < token[:, None])).astype(jnp.bfloat16)
    earlier = jnp.dot(before, hits.astype(jnp.bfloat16), preferred_element_type=jnp.float32)
    row = jnp.arange(plane * blocks * CAP, dtype=jnp.int32)
    row_place = row // (blocks * CAP)
    spread = (row_place[:, None] == place[None, :]).astype(jnp.bfloat16)
    take = lambda v: lax.dot_general(
        spread, v.astype(jnp.bfloat16), (((1,), (1,)), ((), ())), preferred_element_type=jnp.float32
    )
    here = (row // CAP % blocks)[:, None] == own_block[None, :]
    slot = jnp.where(hits > 0, earlier, -1.0)
    chosen = here & (take(slot) == (row % CAP)[:, None].astype(jnp.float32))
    one_hot = chosen.astype(jnp.bfloat16)
    return one_hot, jnp.where(chosen, take(worth), 0.0).astype(jnp.bfloat16)


def shards(tokens, cotangent, route_ids, route_gates, gate_up, down, moment1, moment2, placement):
    tok_rows, width = tokens.shape
    top = route_ids.shape[1]
    hidden_units = down.shape[2]
    groups = lax.axis_size(DP)
    line = lax.axis_size("zl")
    plane = lax.axis_size(PLANE)
    experts = lax.axis_size(EXPERT)
    share = width // groups
    bf16 = jnp.bfloat16

    meta = jnp.concatenate(
        [route_ids.astype(bf16), route_gates, jnp.zeros((tok_rows, META - 2 * top), bf16)], axis=1
    )
    cot_parts = cotangent.reshape(tok_rows, groups, share).transpose(1, 0, 2)
    cot_parts = jnp.concatenate(
        [cot_parts, jnp.broadcast_to(meta[None], (groups, tok_rows, META))], axis=2
    )
    tok_line, cot_line = line_gather(tokens, cot_parts)
    tok_line = tok_line.reshape(line * tok_rows, width)
    own_meta = lax.dynamic_index_in_dim(cot_line[:, :, :, share:], lax.axis_index(DP), 1, keepdims=False)
    own_meta = own_meta.reshape(line * tok_rows, META)
    cot_pack = cot_line.reshape(line * groups * tok_rows, share + META)
    weights = lax.all_gather(gate_up[0], DP, axis=0, tiled=True)

    tok_pick, _ = pickers(own_meta, line, tok_rows, top)
    rows = jnp.dot(tok_pick, tok_line, preferred_element_type=jnp.float32).astype(bf16)
    rows = lax.all_to_all(
        rows.reshape(plane, line * CAP, width), PLANE, split_axis=0, concat_axis=0, tiled=True
    ).reshape(plane * line * CAP, width)

    rows, cot_pack = lax.optimization_barrier((rows, cot_pack))
    _, cot_pick = pickers(cot_pack[:, share:], line * groups, tok_rows, top)
    scaled = jnp.dot(cot_pick, cot_pack[:, :share], preferred_element_type=jnp.float32).astype(bf16)
    scaled = lax.all_to_all(
        scaled.reshape(plane, line * groups * CAP, share), PLANE, split_axis=0, concat_axis=0, tiled=True
    )
    scaled = scaled.reshape(plane * line, groups, CAP, share).transpose(1, 0, 2, 3)
    scaled = scaled.reshape(groups * plane * line * CAP, share)

    pre = jnp.dot(rows, weights, preferred_element_type=jnp.float32)
    hidden = (jax.nn.silu(pre[:, :hidden_units]) * pre[:, hidden_units:]).astype(bf16)
    hidden = lax.all_gather(hidden, DP, axis=0, tiled=True)
    grad = lax.dot_general(scaled, hidden, contract_rows, preferred_element_type=jnp.float32)

    correct_one = 1.0 - BETA_ONE**OPT_STEP
    correct_two = 1.0 - BETA_TWO**OPT_STEP
    first = BETA_ONE * moment1[0].astype(jnp.float32) + (1.0 - BETA_ONE) * grad
    second = BETA_TWO * moment2[0].astype(jnp.float32) + (1.0 - BETA_TWO) * grad * grad
    direction = first / correct_one / (jnp.sqrt(second / correct_two) + ADAM_EPS)
    updated = (down[0].astype(jnp.float32) - LEARN_RATE * direction).astype(bf16)

    block_cols = hidden_units // groups
    piece_rows = share // experts
    pieces = updated.reshape(experts, piece_rows, groups, block_cols).transpose(0, 2, 1, 3)
    pieces = pieces.reshape(experts * groups, CAP, piece_rows * block_cols // CAP)
    spread = lax.all_to_all(pieces, EXPERT + DP, split_axis=0, concat_axis=0, tiled=True)
    spread = spread.reshape(experts, CAP, groups * piece_rows * block_cols // CAP)
    picked = jnp.take(spread, placement, axis=0, mode="clip")
    landed = lax.all_to_all(picked, EXPERT, split_axis=0, concat_axis=0, tiled=True)
    landed = landed.reshape(experts, groups, piece_rows, block_cols).transpose(1, 0, 2, 3)
    return landed.reshape(1, width, block_cols)


def solution(mesh):
    grid = Mesh(mesh.devices.reshape(4, 8, 4, 2, 2), EXPERT + DP)
    every = P(EXPERT + DP, None)
    owned = P(EXPERT, DP, None)
    placed = (every, every, every, every, owned, owned, owned, owned, P())
    return jax.shard_map(
        shards, mesh=grid, in_specs=placed, out_specs=P(EXPERT, None, DP), check_vma=False
    )
```

```python
import jax
import jax.numpy as jnp
from jax import lax
from jax.experimental import pallas as pl
from jax.experimental.pallas import tpu as pltpu
from jax.sharding import Mesh, PartitionSpec as P

OPT_STEP = 2


BETA_ONE = 0.9
BETA_TWO = 0.95
ADAM_EPS = 1e-08
LEARN_RATE = 0.25

DP = ("zh", "core")
PLANE = ("x", "y")
EXPERT = ("x", "zl", "y")
CAP = 2
META = 128

contract_rows = (((0,), (0,)), ((), ()))


LINE = 8
MESH = pl.DeviceIdType.MESH


def tok_kernel(
    tok_ref, tok_all, tok_recv, tok_send, own_sem
):
    at, zh, core = lax.axis_index("zl"), lax.axis_index("zh"), lax.axis_index("core")
    me = zh * 2 + core
    has = (at < LINE - 1, at > 0)
    ids = ({"zl": jnp.minimum(at + 1, LINE - 1)}, {"zl": jnp.maximum(at - 1, 0)})
    partners = []
    for dz, dc in ((0, 1), (1, 0), (1, 1)):
        partners.append(((zh + dz) % 2, (core + dc) % 2))

    barrier = pltpu.get_barrier_semaphore()
    for far in (0, 1):

        @pl.when(has[far])
        def _():
            pl.semaphore_signal(barrier, inc=1, device_id=ids[far], device_id_type=MESH)

    pl.semaphore_wait(barrier, has[0].astype(jnp.int32) + has[1].astype(jnp.int32))

    def hop(out, recv, send, block, far, source=None):
        return pltpu.make_async_remote_copy(
            src_ref=out.at[block] if source is None else source,
            dst_ref=out.at[block],
            send_sem=send.at[far, block],
            recv_sem=recv.at[block],
            device_id=ids[far],
            device_id_type=MESH,
        )

    def first(out, recv, send, source=None):
        for far in (0, 1):

            @pl.when(has[far])
            def _():
                hop(out, recv, send, at, far, source).start()

    def step(out, recv, send, s):
        for far in (0, 1):
            block = at - s if far == 0 else at + s
            there = block >= 0 if far == 0 else block < LINE

            @pl.when(there)
            def _():
                hop(out, recv, send, block, far).wait_recv()

            @pl.when(there & has[far])
            def _():
                hop(out, recv, send, block, far).start()

    def finish(out, recv, send, source=None):
        for s in range(LINE):
            for far in (0, 1):
                block = at - s if far == 0 else at + s
                there = block >= 0 if far == 0 else block < LINE

                @pl.when(there & has[far])
                def _():
                    hop(out, recv, send, block, far, source if s == 0 else None).wait_send()

    own = pltpu.make_async_copy(tok_ref, tok_all.at[at], own_sem.at[0])
    tok = (tok_all, tok_recv, tok_send)
    own.start()
    first(*tok, tok_ref)
    for s in range(1, LINE):
        step(*tok, s)
    own.wait()
    finish(*tok, tok_ref)


def cot_kernel(
    cot_ref, cot_all, cot_recv, cot_send, dp_recv, dp_send, own_sem
):
    at, zh, core = lax.axis_index("zl"), lax.axis_index("zh"), lax.axis_index("core")
    me = zh * 2 + core
    has = (at < LINE - 1, at > 0)
    ids = ({"zl": jnp.minimum(at + 1, LINE - 1)}, {"zl": jnp.maximum(at - 1, 0)})
    partners = []
    for dz, dc in ((0, 1), (1, 0), (1, 1)):
        partners.append(((zh + dz) % 2, (core + dc) % 2))

    barrier = pltpu.get_barrier_semaphore()
    for far in (0, 1):

        @pl.when(has[far])
        def _():
            pl.semaphore_signal(barrier, inc=1, device_id=ids[far], device_id_type=MESH)

    for pz, pc in partners:
        pl.semaphore_signal(barrier, inc=1, device_id={"zh": pz, "core": pc}, device_id_type=MESH)
    pl.semaphore_wait(barrier, 3 + has[0].astype(jnp.int32) + has[1].astype(jnp.int32))

    def hop(out, recv, send, block, far, source=None):
        return pltpu.make_async_remote_copy(
            src_ref=out.at[block] if source is None else source,
            dst_ref=out.at[block],
            send_sem=send.at[far, block],
            recv_sem=recv.at[block],
            device_id=ids[far],
            device_id_type=MESH,
        )

    def first(out, recv, send, source=None):
        for far in (0, 1):

            @pl.when(has[far])
            def _():
                hop(out, recv, send, at, far, source).start()

    def step(out, recv, send, s):
        for far in (0, 1):
            block = at - s if far == 0 else at + s
            there = block >= 0 if far == 0 else block < LINE

            @pl.when(there)
            def _():
                hop(out, recv, send, block, far).wait_recv()

            @pl.when(there & has[far])
            def _():
                hop(out, recv, send, block, far).start()

    def finish(out, recv, send, source=None):
        for s in range(LINE):
            for far in (0, 1):
                block = at - s if far == 0 else at + s
                there = block >= 0 if far == 0 else block < LINE

                @pl.when(there & has[far])
                def _():
                    hop(out, recv, send, block, far, source if s == 0 else None).wait_send()

    own_cot = pltpu.make_async_copy(cot_ref.at[me], cot_all.at[at, me], own_sem.at[0])
    swaps = [
        pltpu.make_async_remote_copy(
            src_ref=cot_ref.at[pz * 2 + pc],
            dst_ref=cot_all.at[at, me],
            send_sem=dp_send.at[k],
            recv_sem=dp_recv.at[k],
            device_id={"zh": pz, "core": pc},
            device_id_type=MESH,
        )
        for k, (pz, pc) in enumerate(partners)
    ]
    cot = (cot_all, cot_recv, cot_send)
    for swap in swaps:
        swap.start()
    own_cot.start()
    for swap in swaps:
        swap.wait()
    own_cot.wait()
    first(*cot)
    for s in range(1, LINE):
        step(*cot, s)
    finish(*cot)


def line_gather(kernel, number, value, extra):
    dma = pltpu.SemaphoreType.DMA
    return pl.pallas_call(
        kernel,
        out_shape=jax.ShapeDtypeStruct((LINE,) + value.shape, value.dtype),
        in_specs=[pl.BlockSpec(memory_space=pltpu.VMEM)],
        out_specs=pl.BlockSpec(memory_space=pltpu.VMEM),
        scratch_shapes=[dma((LINE,)), dma((2, LINE))] + [dma((n,)) for n in extra],
        compiler_params=pltpu.CompilerParams(collective_id=number, has_side_effects=True),
    )(value)


def pickers(meta, blocks, block_rows, top):
    plane = lax.axis_size(PLANE)
    wide = meta.shape[0]
    ids = meta[:, :top].astype(jnp.int32)
    gates = meta[:, top : 2 * top].astype(jnp.float32)
    place = jnp.arange(plane, dtype=jnp.int32)
    y_size = lax.axis_size("y")
    wanted = (place // y_size * lax.axis_size("zl") + lax.axis_index("zl")) * y_size + place % y_size
    match = (ids[:, :, None] == wanted).astype(jnp.float32)
    hits = jnp.sum(match, axis=1)
    worth = jnp.sum(match * gates[:, :, None], axis=1)
    token = jnp.arange(wide, dtype=jnp.int32)
    own_block = token // block_rows
    before = ((own_block[:, None] == own_block[None, :]) & (token[None, :] < token[:, None])).astype(jnp.bfloat16)
    earlier = jnp.dot(before, hits.astype(jnp.bfloat16), preferred_element_type=jnp.float32)
    row = jnp.arange(plane * blocks * CAP, dtype=jnp.int32)
    row_place = row // (blocks * CAP)
    spread = (row_place[:, None] == place[None, :]).astype(jnp.bfloat16)
    take = lambda v: lax.dot_general(
        spread, v.astype(jnp.bfloat16), (((1,), (1,)), ((), ())), preferred_element_type=jnp.float32
    )
    here = (row // CAP % blocks)[:, None] == own_block[None, :]
    slot = jnp.where(hits > 0, earlier, -1.0)
    chosen = here & (take(slot) == (row % CAP)[:, None].astype(jnp.float32))
    one_hot = chosen.astype(jnp.bfloat16)
    return one_hot, jnp.where(chosen, take(worth), 0.0).astype(jnp.bfloat16)


def shards(tokens, cotangent, route_ids, route_gates, gate_up, down, moment1, moment2, placement):
    tok_rows, width = tokens.shape
    top = route_ids.shape[1]
    hidden_units = down.shape[2]
    groups = lax.axis_size(DP)
    line = lax.axis_size("zl")
    plane = lax.axis_size(PLANE)
    experts = lax.axis_size(EXPERT)
    share = width // groups
    bf16 = jnp.bfloat16

    meta = jnp.concatenate(
        [route_ids.astype(bf16), route_gates, jnp.zeros((tok_rows, META - 2 * top), bf16)], axis=1
    )
    cot_parts = cotangent.reshape(tok_rows, groups, share).transpose(1, 0, 2)
    cot_parts = jnp.concatenate(
        [cot_parts, jnp.broadcast_to(meta[None], (groups, tok_rows, META))], axis=2
    )
    tok_pack = line_gather(tok_kernel, 0, jnp.concatenate([tokens, meta], axis=1), (1,))
    tok_pack = tok_pack.reshape(line * tok_rows, width + META)
    weights = lax.all_gather(gate_up[0], DP, axis=0, tiled=True)

    tok_pick, _ = pickers(tok_pack[:, width:], line, tok_rows, top)
    rows = jnp.dot(tok_pick, tok_pack[:, :width], preferred_element_type=jnp.float32).astype(bf16)
    rows = lax.all_to_all(
        rows.reshape(plane, line * CAP, width), PLANE, split_axis=0, concat_axis=0, tiled=True
    ).reshape(plane * line * CAP, width)

    rows, cot_parts = lax.optimization_barrier((rows, cot_parts))
    cot_line = line_gather(cot_kernel, 1, cot_parts, (3, 3, 1))
    cot_pack = cot_line.reshape(line * groups * tok_rows, share + META)
    _, cot_pick = pickers(cot_pack[:, share:], line * groups, tok_rows, top)
    scaled = jnp.dot(cot_pick, cot_pack[:, :share], preferred_element_type=jnp.float32).astype(bf16)
    scaled = lax.all_to_all(
        scaled.reshape(plane, line * groups * CAP, share), PLANE, split_axis=0, concat_axis=0, tiled=True
    )
    scaled = scaled.reshape(plane * line, groups, CAP, share).transpose(1, 0, 2, 3)
    scaled = scaled.reshape(groups * plane * line * CAP, share)

    pre = jnp.dot(rows, weights, preferred_element_type=jnp.float32)
    hidden = (jax.nn.silu(pre[:, :hidden_units]) * pre[:, hidden_units:]).astype(bf16)
    hidden = lax.all_gather(hidden, DP, axis=0, tiled=True)
    grad = lax.dot_general(scaled, hidden, contract_rows, preferred_element_type=jnp.float32)

    correct_one = 1.0 - BETA_ONE**OPT_STEP
    correct_two = 1.0 - BETA_TWO**OPT_STEP
    first = BETA_ONE * moment1[0].astype(jnp.float32) + (1.0 - BETA_ONE) * grad
    second = BETA_TWO * moment2[0].astype(jnp.float32) + (1.0 - BETA_TWO) * grad * grad
    direction = first / correct_one / (jnp.sqrt(second / correct_two) + ADAM_EPS)
    updated = (down[0].astype(jnp.float32) - LEARN_RATE * direction).astype(bf16)

    block_cols = hidden_units // groups
    piece_rows = share // experts
    pieces = updated.reshape(experts, piece_rows, groups, block_cols).transpose(0, 2, 1, 3)
    pieces = pieces.reshape(experts * groups, CAP, piece_rows * block_cols // CAP)
    spread = lax.all_to_all(pieces, EXPERT + DP, split_axis=0, concat_axis=0, tiled=True)
    spread = spread.reshape(experts, CAP, groups * piece_rows * block_cols // CAP)
    picked = jnp.take(spread, placement, axis=0, mode="clip")
    landed = lax.all_to_all(picked, EXPERT, split_axis=0, concat_axis=0, tiled=True)
    landed = landed.reshape(experts, groups, piece_rows, block_cols).transpose(1, 0, 2, 3)
    return landed.reshape(1, width, block_cols)


def solution(mesh):
    grid = Mesh(mesh.devices.reshape(4, 8, 4, 2, 2), EXPERT + DP)
    every = P(EXPERT + DP, None)
    owned = P(EXPERT, DP, None)
    placed = (every, every, every, every, owned, owned, owned, owned, P())
    return jax.shard_map(
        shards, mesh=grid, in_specs=placed, out_specs=P(EXPERT, None, DP), check_vma=False
    )
```
